32 devices in a mesh: tm: 8 (over y, x, core), rows: 4 (over z).
Axes of the slice: x: 2, y: 2, z: 4, core: 2. Of those that a mesh axis runs over, the one named last changes fastest.
Arguments:
- snapshots: bfloat16 [16384, 8192], P('tm', 'rows'), may hold values from -6 to 6
- spod_modes: bfloat16 [64, 2, 4, 8192], P('tm', None, None, 'rows'), may hold values from -0.09375 to 0.09375
- freq_index: int32 [64], replicated, may hold values from 1 to 128, as said below
- seg_offsets: int32 [4096], P('tm'), may hold values from 0 to 2047, as said below
Outputs:
- coefficients: float32 [64, 2, 4, 4096], P('rows', None, None, 'tm')
The draws below stay inside these ranges and needn't reach their ends.
Inputs may be any that keep to these rules, and one draw needn't show every extreme that they name: Frequency f is bin freq_index[f] of a segment of 256 snapshots; values may repeat. Segment n starts at snapshot (n // 512) * 2048 + seg_offsets[n]; snapshots past the last one count as zeros.
All inputs are finite; a program needn't handle non-finite values.
Results may differ from the reference program's by a relative error of at most 0.0003.
Values may be sent and summed in bfloat16 or wider, within the bound.
No kernel may reach another device: no remote copies, remote signals or barrier semaphores. Data moves between devices by JAX's collectives and lax.ppermute only.
A program may use at most 64 MiB of HBM per device.

```python
import math
import jax
import jax.numpy as jnp
from jax import lax

F = 64
M = 4
L = 256
T_DEV = 2048
S_DEV = 512
NT = 16384
NR = 8192
NSEG = 4096
N_TM = 8


def force_ends(key, length, block_len, lowest, highest):
    drawn = jax.random.randint(jax.random.fold_in(key, 1), (length,), lowest, highest + 1, dtype=jnp.int32)
    blocks = length // block_len
    high_pos = jax.random.randint(jax.random.fold_in(key, 2), (blocks,), 0, block_len, dtype=jnp.int32)
    step_pos = jax.random.randint(jax.random.fold_in(key, 3), (blocks,), 0, block_len - 1, dtype=jnp.int32)
    low_pos = (high_pos + 1 + step_pos) % block_len
    positions = jnp.arange(length, dtype=jnp.int32)
    within = positions % block_len
    owners = positions // block_len
    result = jnp.where(within == high_pos[owners], highest, drawn)
    return jnp.where(within == low_pos[owners], lowest, result).astype(jnp.int32)


def draw_freq_index(key, part):
    return force_ends(jax.random.fold_in(key, 11), F, F, 1, L // 2)


def draw_seg_offsets(key, part):
    return force_ends(jax.random.fold_in(key, 23), NSEG, S_DEV, 0, T_DEV - 1)


def with_spikes(entries, key, source, target, blocks, factor):
    owner, partner = [(jnp.arange(entries.shape[dim]) // (entries.shape[dim] // blocks)).reshape([-1 if axis == dim else 1 for axis in range(entries.ndim)]) for dim in (source, target)]
    chosen = jax.random.permutation(key, blocks)[partner]
    strong = (owner == chosen) | (owner == (partner + blocks // 2) % blocks)
    return jnp.where(strong, factor * entries, entries)


def levels(own_key, dims, shards, low, top_value):
    def one(axis_at, parts):
        steps = jax.random.uniform(jax.random.fold_in(jax.random.fold_in(own_key, 6), axis_at), (parts,), jnp.float32, low / len(shards), top_value / len(shards))
        return jnp.repeat(jnp.exp(steps), dims[axis_at] // parts).reshape((-1,) + (1,) * (len(dims) - axis_at - 1))

    loudness = one(*shards[0])
    for cut in shards[1:]:
        loudness = loudness * one(*cut)
    return loudness


def normal_values(stream_key, shape, deviation, reach, cuts=(), kind=jnp.bfloat16):
    gain = levels(stream_key, shape, cuts, -0.22, 0.18) if cuts else 1.0
    entries = jax.random.normal(stream_key, shape, jnp.float32) * deviation * gain
    return jnp.minimum(jnp.maximum(entries, -reach), reach).astype(kind)


def gaussian_with(rng, extent, deviation, most, shards, heavy, kind=jnp.bfloat16):
    values = deviation * jax.random.normal(rng, extent, jnp.float32)
    if shards:
        values = values * levels(rng, extent, shards, -0.22, 0.18)
    return jnp.clip(with_spikes(values, jax.random.fold_in(rng, 3), *heavy), -most, most).astype(kind)


def setup_inputs(seed: int = 0) -> dict:
    seeds = jax.random.split(jax.random.key(seed), 5)
    return {
        "snapshots": normal_values(seeds[0], (NT, NR), 1.0, 6.0, ((0, 8), (1, 4))),
        "spod_modes": gaussian_with(seeds[1], (F, 2, M, NR), NR ** -0.5, 0.09375, ((0, 8), (3, 4)), (3, 0, 8, 2.0)),
        "freq_index": draw_freq_index(jax.random.fold_in(seeds[4], 71), 0),
        "seg_offsets": draw_seg_offsets(jax.random.fold_in(seeds[4], 71), 0),
    }


def hann_weights(distance):
    inside = (distance >= 0) & (distance < L)
    angles = distance.astype(jnp.float32) * (2.0 * math.pi / L)
    values = math.sqrt(8.0 / (3.0 * L)) * (0.5 - 0.5 * jnp.cos(angles))
    return jnp.where(inside, values, 0.0).astype(jnp.float32)

def phase_pair(frequency, moments):
    phase_bin = frequency[:, None] * moments[None, :] % L
    angles = phase_bin.astype(jnp.float32) * (2.0 * math.pi / L)
    return (jnp.cos(angles)[:, None, :], jnp.sin(angles)[:, None, :])

def demodulate(projected, frequency, moments):
    cosine, sine_part = phase_pair(frequency, moments)
    real_in = projected[:, 0]
    imag_in = projected[:, 1]
    real_out = cosine * real_in - sine_part * imag_in
    imag_out = -(sine_part * real_in + cosine * imag_in)
    return jnp.stack([real_out, imag_out], 1).astype(jnp.float32)

def envelope(extended, offsets, frequency, base_time):
    distance = jnp.arange(extended.shape[3], dtype=jnp.int32)[None, :] - offsets[:, None]
    weights = hann_weights(distance)
    groups = extended.shape[0]
    flat_rows = extended.reshape(groups * extended.shape[1] * extended.shape[2], extended.shape[3])
    summed = lax.dot_general(flat_rows, weights, (((1,), (1,)), ((), ())), precision=lax.Precision.HIGHEST, preferred_element_type=jnp.float32)
    summed = summed.reshape(groups, 2, extended.shape[2], offsets.shape[0])
    cosine, sine_part = phase_pair(frequency, base_time + offsets)
    env_real = summed[:, 0]
    env_imag = summed[:, 1]
    return jnp.stack([cosine * env_real - sine_part * env_imag, sine_part * env_real + cosine * env_imag], 1)

def reference(snapshots, spod_modes, freq_index, seg_offsets):
    flat_modes = spod_modes.reshape(F * 2 * M, NR)
    projected = lax.dot_general(flat_modes, snapshots, (((1,), (1,)), ((), ())), preferred_element_type=jnp.float32)
    projected = projected.reshape(F, 2, M, NT)
    demodulated = demodulate(projected, freq_index, jnp.arange(NT, dtype=jnp.int32))
    padded = jnp.concatenate([demodulated, jnp.zeros((F, 2, M, L), jnp.float32)], 3)

    def one_block(block_id):
        extended = lax.dynamic_slice_in_dim(padded, (block_id * T_DEV).astype(jnp.int32), T_DEV + L, 3)
        offsets = lax.dynamic_slice_in_dim(seg_offsets, (block_id * S_DEV).astype(jnp.int32), S_DEV, 0)
        return envelope(extended, offsets, freq_index, (block_id * T_DEV).astype(jnp.int32))
    blocks = lax.map(one_block, jnp.arange(N_TM, dtype=jnp.int32))
    return jnp.moveaxis(blocks, 0, 3).reshape(F, 2, M, NSEG)
```

```python
import functools
import math

import jax
import jax.numpy as jnp
from jax import lax
from jax.experimental import pallas as pl
from jax.experimental.pallas import tpu as pltpu
from jax.sharding import PartitionSpec as P

M = 4
L = 256
ROWS = 2 * M
EXTRA = 16
TOP = 32000.0


def swap(block, axis, distance):
    return lax.ppermute(block, axis, [(i, i ^ distance) for i in range(lax.axis_size(axis))])


def phase_pair(frequency, moments):
    phase_bin = frequency[:, None] * moments[None, :] % L
    angles = phase_bin.astype(jnp.float32) * (2.0 * math.pi / L)
    return jnp.cos(angles), jnp.sin(angles)


def split(value):
    high = value.astype(jnp.bfloat16)
    return high, (value - high.astype(jnp.float32)).astype(jnp.bfloat16)


def dot(a, b, contract=((1,), (0,))):
    return lax.dot_general(a, b, (contract, ((), ())), preferred_element_type=jnp.float32)


def product3(data_high, data_low, weights_high, weights_low):
    return dot(data_high, weights_high) + dot(data_low, weights_high) + dot(data_high, weights_low)


def weights_kernel(offsets_ref, high_ref, low_ref, base_high, base_low):
    step = pl.program_id(0)
    shape = base_high.shape
    moment = lax.broadcasted_iota(jnp.int32, shape, 0)
    offsets = offsets_ref[...]

    @pl.when(step == 0)
    def _():
        angles = ((moment - offsets) & (L - 1)).astype(jnp.float32) * (2.0 * math.pi / L)
        values = math.sqrt(8.0 / (3.0 * L)) * (0.5 - 0.5 * jnp.cos(angles))
        high = values.astype(jnp.bfloat16).astype(jnp.float32)
        base_high[...] = high
        base_low[...] = values - high

    distance = moment + step * L - offsets
    inside = (distance >= 0) & (distance < L)
    high_ref[...] = jnp.where(inside, base_high[...], 0.0).astype(jnp.bfloat16)
    low_ref[...] = jnp.where(inside, base_low[...], 0.0).astype(jnp.bfloat16)


def window_weights(offsets, blocks):
    count = offsets.shape[0]
    kind = jax.ShapeDtypeStruct((blocks * L, count), jnp.bfloat16)
    spec = pl.BlockSpec((L, count), lambda i: (i, 0))
    return pl.pallas_call(
        weights_kernel,
        out_shape=(kind, kind),
        grid=(blocks,),
        in_specs=[pl.BlockSpec((1, count), lambda i: (0, 0))],
        out_specs=(spec, spec),
        scratch_shapes=[pltpu.VMEM((L, count), jnp.float32)] * 2,
        name="weights",
    )(offsets[None, :])


def turn(x, cosine, sine, first, second):
    return first * cosine * x + second * sine * pltpu.roll(x, M, 0)


def signs(width):
    real = lax.broadcasted_iota(jnp.int32, (ROWS, width), 0) < M
    return jnp.where(real, 1.0, -1.0).astype(jnp.float32)


def head_kernel(modes_ref, snaps_ref, cos_ref, sin_ref, out_ref):
    out_ref[...] = dot(modes_ref[...], snaps_ref[...], ((1,), (1,)))
    sign = signs(L)
    for f in range(cos_ref.shape[0]):
        rows = slice(f * ROWS, (f + 1) * ROWS)
        out_ref[rows, :] = turn(out_ref[rows, :], cos_ref[f : f + 1, :], sin_ref[f : f + 1, :], sign, -1.0)


def head(modes, snapshots, cosine, sine):
    rows = modes.shape[0]
    return pl.pallas_call(
        head_kernel,
        out_shape=jax.ShapeDtypeStruct((rows, L), jnp.float32),
        grid=(1,),
        in_specs=[
            pl.BlockSpec(modes.shape, lambda i: (0, 0)),
            pl.BlockSpec((L, snapshots.shape[1]), lambda i: (0, 0)),
            pl.BlockSpec((cosine.shape[0], L), lambda i: (0, 0)),
            pl.BlockSpec((cosine.shape[0], L), lambda i: (0, 0)),
        ],
        out_specs=pl.BlockSpec((rows, L), lambda i: (0, 0)),
        name="head",
    )(modes, snapshots, cosine, sine)


def main_kernel(modes_ref, snaps_ref, cos_ref, sin_ref, wh_ref, wl_ref, acc_ref, high_ref, low_ref):
    projected = dot(modes_ref[...], snaps_ref[...], ((1,), (1,)))
    sign = signs(L)
    for g in range(cos_ref.shape[0] // 2):
        parts = []
        for f in (2 * g, 2 * g + 1):
            x = projected[f * ROWS : (f + 1) * ROWS, :]
            parts.append(turn(x, cos_ref[f : f + 1, :], sin_ref[f : f + 1, :], sign, -1.0))
        both = jnp.concatenate(parts, 0)
        rows = slice(2 * g * ROWS, (2 * g + 2) * ROWS)
        high_ref[rows, :], low_ref[rows, :] = split(both)
    part = product3(high_ref[...], low_ref[...], wh_ref[...], wl_ref[...])

    @pl.when(pl.program_id(0) == 0)
    def _():
        acc_ref[...] = part

    @pl.when(pl.program_id(0) > 0)
    def _():
        acc_ref[...] += part


def envelopes(modes, snapshots, cosine, sine, high, low):
    rows, depth = modes.shape
    count = high.shape[1]
    table = pl.BlockSpec((cosine.shape[0], L), lambda i: (0, i))
    window = pl.BlockSpec((L, count), lambda i: (i, 0))
    return pl.pallas_call(
        main_kernel,
        out_shape=jax.ShapeDtypeStruct((rows, count), jnp.float32),
        grid=(snapshots.shape[0] // L,),
        in_specs=[
            pl.BlockSpec((rows, depth), lambda i: (0, 0)),
            pl.BlockSpec((L, depth), lambda i: (i, 0)),
            table,
            table,
            window,
            window,
        ],
        out_specs=pl.BlockSpec((rows, count), lambda i: (0, 0)),
        scratch_shapes=[pltpu.VMEM((rows, L), jnp.bfloat16)] * 2,
        name="envelopes",
    )(modes, snapshots, cosine, sine, high, low)


def code_kernel(per_dest, place_ref, acc_ref, halo_ref, wh_ref, wl_ref, cos_ref, sin_ref, own_ref, *rest):
    code_refs, full_ref, chunk_ref, turned_ref = rest[:-3], rest[-3], rest[-2], rest[-1]
    tm_pos, row_pos, shift = place_ref[0], place_ref[1], place_ref[2]
    count = acc_ref.shape[1]
    chunk = own_ref.shape[0]
    block = chunk // per_dest
    for d in range(halo_ref.shape[0] // block):
        at = pl.multiple_of((d ^ shift) * block, ROWS)
        turned_ref[d * block : (d + 1) * block, :] = halo_ref[pl.ds(at, block), :]
    high, low = split(turned_ref[...])
    full_ref[...] = acc_ref[...] + product3(high, low, wh_ref[...], wl_ref[...])
    sign = signs(count)
    for f in range(cos_ref.shape[0]):
        rows = slice(f * ROWS, (f + 1) * ROWS)
        full_ref[rows, :] = turn(full_ref[rows, :], cos_ref[f : f + 1, :], sin_ref[f : f + 1, :], 1.0, -sign)
    for k in range(len(code_refs) + 1):
        target = own_ref if k == 0 else chunk_ref
        for u in range(per_dest):
            at = (((row_pos ^ k) * per_dest + u) ^ tm_pos) * block
            target[u * block : (u + 1) * block, :] = full_ref[pl.ds(pl.multiple_of(at, ROWS), block), :]
        if k > 0:
            code_ref = code_refs[k - 1]
            values = chunk_ref[...]
            peak = jnp.max(jnp.abs(values), axis=1, keepdims=True)
            power = jnp.ceil(jnp.log2(jnp.maximum(peak * (1.0 / TOP), 2.0**-126)))
            power = jnp.maximum(power, -126.0)
            codes = jnp.round(values * jnp.exp2(-power))
            code_ref[:chunk, :] = codes.astype(jnp.int32).astype(jnp.int16)
            here = lax.broadcasted_iota(jnp.int32, (chunk, count), 0)
            there = lax.broadcasted_iota(jnp.int32, (chunk, count), 1)
            line = jnp.sum(jnp.where(here == there, power, 0.0), axis=0, keepdims=True)
            line = jnp.broadcast_to(line, (EXTRA, count)).astype(jnp.int32)
            code_ref[chunk:, :] = line.astype(jnp.int16)


def rotate_and_code(place, acc, halo, high, low, cosine, sine, chunk, sends, per_dest):
    rows, count = acc.shape
    last = high.shape[0] // L - 1
    whole = lambda shape: pl.BlockSpec(shape, lambda i, p: (0,) * len(shape))
    window = pl.BlockSpec((L, count), lambda i, p: (last, 0))
    code = jax.ShapeDtypeStruct((chunk + EXTRA, count), jnp.int16)
    return pl.pallas_call(
        functools.partial(code_kernel, per_dest),
        out_shape=(jax.ShapeDtypeStruct((chunk, count), jnp.float32),) + (code,) * sends,
        grid_spec=pltpu.PrefetchScalarGridSpec(
            num_scalar_prefetch=1,
            grid=(1,),
            in_specs=[whole(acc.shape), whole(halo.shape), window, window, whole(cosine.shape), whole(sine.shape)],
            out_specs=(whole((chunk, count)),) + (whole((chunk + EXTRA, count)),) * sends,
            scratch_shapes=[pltpu.VMEM((rows, count), jnp.float32), pltpu.VMEM((chunk, count), jnp.float32), pltpu.VMEM(halo.shape, jnp.float32)],
        ),
        name="rotate_and_code",
    )(place, acc, halo, high, low, cosine, sine)


def sum_kernel(own_ref, *refs):
    code_refs, out_ref = refs[:-1], refs[-1]
    chunk, count = own_ref.shape
    total = own_ref[...]
    here = lax.broadcasted_iota(jnp.int32, (chunk, count), 0)
    there = lax.broadcasted_iota(jnp.int32, (chunk, count), 1)
    for ref in code_refs:
        line = ref[chunk:, :].astype(jnp.int32).astype(jnp.float32)[0:1, :]
        power = jnp.sum(jnp.where(here == there, line, 0.0), axis=1, keepdims=True)
        total = total + ref[:chunk, :].astype(jnp.int32).astype(jnp.float32) * jnp.exp2(power)
    for f in range(out_ref.shape[0]):
        for p in range(2):
            at = f * ROWS + p * M
            out_ref[f, p] = total[at : at + M, :]


def add_up(own, codes):
    chunk, count = own.shape
    return pl.pallas_call(
        sum_kernel,
        out_shape=jax.ShapeDtypeStruct((chunk // ROWS, 2, M, count), jnp.float32),
        name="add_up",
    )(own, *codes)


def body(snapshots, spod_modes, freq_index, seg_offsets):
    time_len = snapshots.shape[0]
    tm_pos = lax.axis_index("tm")
    row_pos = lax.axis_index("rows")
    n_tm = lax.axis_size("tm")
    n_rows = lax.axis_size("rows")
    per_device = spod_modes.shape[0]
    groups = n_tm * per_device
    chunk = groups // n_rows * ROWS

    blocks = {0: spod_modes.reshape(per_device * ROWS, spod_modes.shape[3])}
    for d in range(2, n_tm, 2):
        blocks[d] = swap(blocks[0], "tm", d)
    for d in range(0, n_tm, 2):
        blocks[d + 1] = swap(blocks[d], "tm", 1)
    modes = jnp.concatenate([blocks[d] for d in range(n_tm)], 0)

    order = jnp.arange(n_tm, dtype=jnp.int32) ^ tm_pos
    frequency = freq_index.reshape(n_tm, per_device)[order].reshape(groups)
    base_time = tm_pos * time_len
    cosine, sine = phase_pair(frequency, base_time + jnp.arange(time_len, dtype=jnp.int32))
    seg_cosine, seg_sine = phase_pair(frequency, base_time + seg_offsets)
    high, low = window_weights(seg_offsets, time_len // L + 1)

    first = head(modes, snapshots, cosine, sine)
    halo = lax.ppermute(first, "tm", [(i + 1, i) for i in range(n_tm - 1)])

    acc = envelopes(modes, snapshots, cosine, sine, high, low)
    place = jnp.stack([tm_pos, row_pos, (tm_pos ^ (tm_pos + 1)) & (n_tm - 1)]).astype(jnp.int32)
    own, *codes = rotate_and_code(place, acc, halo, high, low, seg_cosine, seg_sine, chunk, n_rows - 1, n_tm // n_rows)
    codes = [swap(code, "rows", k + 1) for k, code in enumerate(codes)]
    return add_up(own, codes)


def solution(mesh):
    placed = (P("tm", "rows"), P("tm", None, None, "rows"), P(), P("tm"))
    return jax.shard_map(
        body, mesh=mesh, in_specs=placed, out_specs=P("rows", None, None, "tm"), check_vma=False
    )
```

```python
import functools
import math

import jax
import jax.numpy as jnp
from jax import lax
from jax.experimental import pallas as pl
from jax.experimental.pallas import tpu as pltpu
from jax.sharding import PartitionSpec as P

M = 4
L = 256
ROWS = 2 * M
TOP = 32000.0
SPAN = 512
LANES = 128


def swap(block, axis, distance):
    return lax.ppermute(block, axis, [(i, i ^ distance) for i in range(lax.axis_size(axis))])


def split(value):
    high = value.astype(jnp.bfloat16)
    return high, (value - high.astype(jnp.float32)).astype(jnp.bfloat16)


def dot(a, b, contract=((1,), (0,))):
    return lax.dot_general(a, b, (contract, ((), ())), preferred_element_type=jnp.float32)


def product3(data_high, data_low, weights_high, weights_low):
    return dot(data_high, weights_high) + dot(data_low, weights_high) + dot(data_high, weights_low)


def turn(x, cosine, sine, first, second):
    return first * cosine * x + second * sine * pltpu.roll(x, M, 0)


def signs(width):
    real = lax.broadcasted_iota(jnp.int32, (ROWS, width), 0) < M
    return jnp.where(real, 1.0, -1.0).astype(jnp.float32)


def whole(shape):
    return pl.BlockSpec(shape, lambda *_: (0,) * len(shape))


def angle(phase_bin):
    return (phase_bin & (L - 1)).astype(jnp.float32) * (2.0 * math.pi / L)


def tables_kernel(offsets_ref, frequency_ref, high_ref, low_ref, cos_ref, sin_ref, seg_cos_ref, seg_sin_ref, *bases):
    step = pl.program_id(0)
    distance_ref, base_high, base_low = bases

    @pl.when(step == 0)
    def _():
        shape = base_high.shape
        distance = lax.broadcasted_iota(jnp.int32, shape, 0) - offsets_ref[...]
        values = math.sqrt(8.0 / (3.0 * L)) * (0.5 - 0.5 * jnp.cos(angle(distance)))
        base_high[...], base_low[...] = split(values)
        distance_ref[...] = distance.astype(jnp.int16)
        theta = angle(frequency_ref[...] * lax.broadcasted_iota(jnp.int32, cos_ref.shape, 1))
        cos_ref[...] = jnp.cos(theta)
        sin_ref[...] = jnp.sin(theta)
        phi = angle(frequency_ref[...] * offsets_ref[...])
        seg_cos_ref[...] = jnp.cos(phi)
        seg_sin_ref[...] = jnp.sin(phi)

    distance = distance_ref[...] + (step * L).astype(jnp.int16)
    inside = (distance >= 0) & (distance < L)
    none = jnp.zeros(base_high.shape, jnp.bfloat16)
    high_ref[...] = jnp.where(inside, base_high[...], none)
    low_ref[...] = jnp.where(inside, base_low[...], none)


def tables(offsets, frequency, blocks):
    count, groups = offsets.shape[0], frequency.shape[0]
    weights = jax.ShapeDtypeStruct((blocks * L, count), jnp.bfloat16)
    window = pl.BlockSpec((L, count), lambda i: (i, 0))
    theta = jax.ShapeDtypeStruct((groups, L), jnp.float32)
    phi = jax.ShapeDtypeStruct((groups, count), jnp.float32)
    return pl.pallas_call(
        tables_kernel,
        out_shape=(weights, weights, theta, theta, phi, phi),
        grid=(blocks,),
        in_specs=[whole((1, count)), whole((groups, 1))],
        out_specs=(window, window) + (whole((groups, L)),) * 2 + (whole((groups, count)),) * 2,
        scratch_shapes=[pltpu.VMEM((L, count), kind) for kind in (jnp.int16, jnp.bfloat16, jnp.bfloat16)],
        name="tables",
    )(offsets[None, :], frequency[:, None])


def span_kernel(pieces, first, *refs):
    refs = list(refs)
    piece_refs, refs = refs[:pieces], refs[pieces:]
    snaps_ref, cos_ref, sin_ref, wh_ref, wl_ref = refs[:5]
    refs = refs[5:]
    before_ref = None if first else refs.pop(0)
    acc_ref = refs.pop(0)
    head_ref = refs.pop(0) if first else None
    modes_ref, high_ref, low_ref = refs
    step = pl.program_id(0)

    @pl.when(step == 0)
    def _():
        at = 0
        for ref in piece_refs:
            modes_ref[at : at + ref.shape[0], :] = ref[...]
            at += ref.shape[0]

    projected = dot(modes_ref[...], snaps_ref[...], ((1,), (1,)))
    sign = signs(L)
    for g in range(cos_ref.shape[0] // 2):
        rows = slice(2 * g * ROWS, (2 * g + 2) * ROWS)
        factors = [(sign * cos_ref[f : f + 1, :], -sin_ref[f : f + 1, :]) for f in (2 * g, 2 * g + 1)]
        for b in range(high_ref.shape[1] // L):
            cols = slice(b * L, (b + 1) * L)
            parts = []
            for u, (cosine, sine) in enumerate(factors):
                f = 2 * g + u
                x = projected[f * ROWS : (f + 1) * ROWS, cols]
                parts.append(cosine * x + sine * pltpu.roll(x, M, 0))
            both = jnp.concatenate(parts, 0)
            if first and b == 0:
                head_ref[rows, :] = both
            high_ref[rows, cols], low_ref[rows, cols] = split(both)
    part = product3(high_ref[...], low_ref[...], wh_ref[...], wl_ref[...])

    if first:
        acc_ref[...] = part
    else:

        @pl.when(step == 0)
        def _():
            acc_ref[...] = before_ref[...] + part

        @pl.when(step > 0)
        def _():
            acc_ref[...] += part


def spans(stage, pieces, snapshots, angles, high, low, start, steps, span, before=None):
    depth = snapshots.shape[1]
    rows = sum(piece.shape[0] for piece in pieces)
    count = high.shape[1]
    first = before is None
    table = pl.BlockSpec((rows // ROWS, L), lambda i: (stage, 0))
    window = pl.BlockSpec((span, count), lambda i: (i + start, 0))
    acc = jax.ShapeDtypeStruct((rows, count), jnp.float32)
    head = jax.ShapeDtypeStruct((rows, L), jnp.float32)
    return pl.pallas_call(
        functools.partial(span_kernel, len(pieces), first),
        out_shape=(acc, head) if first else acc,
        grid=(steps,),
        in_specs=[whole(piece.shape) for piece in pieces]
        + [pl.BlockSpec((span, depth), lambda i: (i + start, 0))]
        + [table, table, window, window]
        + ([] if first else [whole(acc.shape)]),
        out_specs=(whole(acc.shape), whole(head.shape)) if first else whole(acc.shape),
        scratch_shapes=[pltpu.VMEM((rows, depth), jnp.bfloat16)] + [pltpu.VMEM((rows, span), jnp.bfloat16)] * 2,
        name="first_span" if first else "other_spans",
    )(*pieces, snapshots, *angles[:2], high, low, *([] if first else [before]))


def code_kernel(per_dest, place_ref, acc_ref, halo_ref, wh_ref, wl_ref, cos_ref, sin_ref, own_ref, *rest):
    code_refs, full_ref, turned_ref = rest[:-2], rest[-2], rest[-1]
    tm_pos, row_pos, shift = place_ref[0], place_ref[1], place_ref[2]
    chunk, count = own_ref.shape
    block = chunk // per_dest
    half = halo_ref.shape[0] // block // 2

    def row_of(distance):
        return pl.multiple_of((distance // 2 + (distance & 1) * half) * block, ROWS)

    for d in range(2 * half):
        at = (d // 2 + (d & 1) * half) * block
        turned_ref[at : at + block, :] = halo_ref[pl.ds(row_of(d ^ shift), block), :]
    high, low = split(turned_ref[...])
    full_ref[...] = acc_ref[...] + product3(high, low, wh_ref[...], wl_ref[...])
    sign = signs(count)
    for f in range(cos_ref.shape[0]):
        rows = slice(f * ROWS, (f + 1) * ROWS)
        full_ref[rows, :] = turn(full_ref[rows, :], cos_ref[f : f + 1, :], sin_ref[f : f + 1, :], 1.0, -sign)
    lane = lax.broadcasted_iota(jnp.int32, (2 * ROWS, LANES), 1)
    for k in range(len(code_refs) + 1):
        for u in range(per_dest):
            at = row_of(((row_pos ^ k) * per_dest + u) ^ tm_pos)
            for r in range(0, block, 2 * ROWS):
                values = full_ref[pl.ds(pl.multiple_of(at + r, ROWS), 2 * ROWS), :]
                rows = slice(u * block + r, u * block + r + 2 * ROWS)
                if k == 0:
                    own_ref[rows, :] = values
                    continue
                peak = jnp.max(jnp.abs(values), axis=1, keepdims=True)
                power = jnp.ceil(jnp.log2(jnp.maximum(peak * (1.0 / TOP), 2.0**-126)))
                power = jnp.maximum(power, -126.0)
                codes = jnp.round(values * jnp.exp2(-power)).astype(jnp.int32)
                bits = lax.shift_right_logical(jnp.broadcast_to(power.astype(jnp.int32) + 127, lane.shape), lane & 7) & 1
                front = codes[:, :LANES]
                front = jnp.where(lane < 8, (front & -2) | bits, front)
                code_refs[k - 1][rows, :LANES] = front.astype(jnp.int16)
                code_refs[k - 1][rows, LANES:] = codes[:, LANES:].astype(jnp.int16)


def rotate_and_code(stage, place, acc, halo, high, low, angles, chunk, sends, per_dest):
    rows, count = acc.shape
    last = high.shape[0] // L - 1
    window = pl.BlockSpec((L, count), lambda i, p: (last, 0))
    table = pl.BlockSpec((rows // ROWS, count), lambda i, p: (stage, 0))
    code = jax.ShapeDtypeStruct((chunk, count), jnp.int16)
    return pl.pallas_call(
        functools.partial(code_kernel, per_dest),
        out_shape=(jax.ShapeDtypeStruct((chunk, count), jnp.float32),) + (code,) * sends,
        grid_spec=pltpu.PrefetchScalarGridSpec(
            num_scalar_prefetch=1,
            grid=(1,),
            in_specs=[whole(acc.shape), whole(halo.shape), window, window, table, table],
            out_specs=(whole((chunk, count)),) * (sends + 1),
            scratch_shapes=[pltpu.VMEM((rows, count), jnp.float32), pltpu.VMEM(halo.shape, jnp.float32)],
        ),
        name="rotate_and_code",
    )(place, acc, halo, high, low, *angles[2:])


def sum_kernel(stages, per_dest, *refs):
    out_ref = refs[-1]
    sends = (len(refs) - 1) // stages - 1
    block = refs[0].shape[0] // per_dest
    lane = lax.broadcasted_iota(jnp.int32, (block, LANES), 1)
    for s in range(stages):
        own_ref, code_refs = refs[s * (sends + 1)], refs[s * (sends + 1) + 1 : (s + 1) * (sends + 1)]
        for u in range(per_dest):
            rows = slice(u * block, (u + 1) * block)
            total = own_ref[rows, :]
            for ref in code_refs:
                codes = ref[rows, :].astype(jnp.int32)
                bits = jnp.where(lane < 8, (codes[:, :LANES] & 1) << (lane & 7), 0)
                power = jnp.sum(bits.astype(jnp.float32), axis=1, keepdims=True) - 127.0
                total = total + codes.astype(jnp.float32) * jnp.exp2(power)
            for f in range(block // ROWS):
                for p in range(2):
                    at = f * ROWS + p * M
                    out_ref[(u * stages + s) * (block // ROWS) + f, p] = total[at : at + M, :]


def add_up(stages, per_dest, parts):
    chunk, count = parts[0].shape
    return pl.pallas_call(
        functools.partial(sum_kernel, stages, per_dest),
        out_shape=jax.ShapeDtypeStruct((stages * chunk // ROWS, 2, M, count), jnp.float32),
        name="add_up",
    )(*parts)


def others(own):
    return [own] + [swap(own, "tm", d) for d in range(2, lax.axis_size("tm"), 2)]


def after(values, earlier):
    return list(lax.optimization_barrier((*values, earlier)))[:-1]


def body(snapshots, spod_modes, freq_index, seg_offsets):
    time_len = snapshots.shape[0]
    tm_pos = lax.axis_index("tm")
    row_pos = lax.axis_index("rows")
    n_tm = lax.axis_size("tm")
    n_rows = lax.axis_size("rows")
    per_device = spod_modes.shape[0]
    groups = n_tm * per_device
    stages = 2 if per_device % 4 == 0 else 1
    per_stage = per_device // stages
    chunk = n_tm // n_rows * per_stage * ROWS
    span = math.gcd(SPAN, time_len)

    flat = spod_modes.reshape(stages, per_stage * ROWS, spod_modes.shape[3])
    even = [others(flat[s]) for s in range(stages)]

    order = jnp.arange(n_tm, dtype=jnp.int32).reshape(n_tm // 2, 2).T.reshape(n_tm) ^ tm_pos
    frequency = freq_index.reshape(n_tm, stages, per_stage)[order].swapaxes(0, 1).reshape(groups)
    place = jnp.stack([tm_pos, row_pos, (tm_pos ^ (tm_pos + 1)) & (n_tm - 1)]).astype(jnp.int32)
    high, low, *angles = tables(seg_offsets, frequency, time_len // L + 1)
    [snapshots] = after([snapshots], place)

    parts = []
    for s in range(stages):
        pieces = even[s] + [swap(block, "tm", 1) for block in even[s]]
        acc, head = spans(s, pieces, snapshots, angles, high, low, 0, 1, span)
        if s + 1 < stages:
            even[s + 1] = after(even[s + 1], head)
        halo = lax.ppermute(head, "tm", [(i + 1, i) for i in range(n_tm - 1)])
        acc = spans(s, pieces, snapshots, angles, high, low, 1, time_len // span - 1, span, before=acc)
        own, *codes = rotate_and_code(s, place, acc, halo, high, low, angles, chunk, n_rows - 1, n_tm // n_rows)
        [snapshots] = after([snapshots], own)
        parts += [own] + [swap(code, "rows", k + 1) for k, code in enumerate(codes)]
    return add_up(stages, n_tm // n_rows, parts)


def solution(mesh):
    placed = (P("tm", "rows"), P("tm", None, None, "rows"), P(), P("tm"))
    return jax.shard_map(
        body, mesh=mesh, in_specs=placed, out_specs=P("rows", None, None, "tm"), check_vma=False
    )
```

```python
import functools
import math

import jax
import jax.numpy as jnp
from jax import lax
from jax.experimental import pallas as pl
from jax.experimental.pallas import tpu as pltpu
from jax.sharding import PartitionSpec as P

M = 4
L = 256
ROWS = 2 * M
TOP = 32000.0
SPAN = 512
LANES = 128
MAGIC = 12582912.0


def swap(block, axis, distance):
    return lax.ppermute(block, axis, [(i, i ^ distance) for i in range(lax.axis_size(axis))])


def split(value):
    high = value.astype(jnp.bfloat16)
    return high, (value - high.astype(jnp.float32)).astype(jnp.bfloat16)


def dot(a, b, contract=((1,), (0,))):
    return lax.dot_general(a, b, (contract, ((), ())), preferred_element_type=jnp.float32)


def product3(data_high, data_low, weights_high, weights_low):
    return dot(data_high, weights_high) + dot(data_low, weights_high) + dot(data_high, weights_low)


def signs(width):
    real = lax.broadcasted_iota(jnp.int32, (ROWS, width), 0) < M
    return jnp.where(real, 1.0, -1.0).astype(jnp.float32)


VMEM = pl.BlockSpec(memory_space=pltpu.VMEM)
PARAMS = pltpu.CompilerParams(vmem_limit_bytes=20 * 2**20)


def kept(shape, kind):
    return pltpu.VMEM(shape, kind)


def hold(*values):
    return [pltpu.with_memory_space_constraint(value, pltpu.VMEM) for value in values]


def half_sine(phase_bin):
    centred = ((phase_bin + L // 2) & (L - 1)) - L // 2
    u = centred.astype(jnp.float32) * (math.pi / L)
    square = u * u
    sine = jnp.full_like(u, -1.0 / math.factorial(11))
    for k in (9, 7, 5, 3, 1):
        sine = sine * square + (-1.0) ** (k // 2) / math.factorial(k)
    return u, square, u * sine


def cos_sin(phase_bin):
    u, square, sine = half_sine(phase_bin)
    cosine = jnp.full_like(u, 1.0 / math.factorial(12))
    for k in (10, 8, 6, 4, 2, 0):
        cosine = cosine * square + (-1.0) ** (k // 2) / math.factorial(k)
    return 1.0 - 2.0 * sine * sine, 2.0 * sine * cosine


def tables_kernel(offsets_ref, frequency_ref, high_ref, low_ref, cos_ref, sin_ref, seg_cos_ref, seg_sin_ref, *bases):
    distance_ref, base_high, base_low = bases
    shape = base_high.shape
    distance = lax.broadcasted_iota(jnp.int32, shape, 0) - offsets_ref[...]
    _, _, sine = half_sine(distance)
    base_high[...], base_low[...] = split(math.sqrt(8.0 / (3.0 * L)) * (sine * sine))
    distance_ref[...] = distance.astype(jnp.int16)
    cos_ref[...], sin_ref[...] = cos_sin(frequency_ref[...] * lax.broadcasted_iota(jnp.int32, cos_ref.shape, 1))
    seg_cos_ref[...], seg_sin_ref[...] = cos_sin(frequency_ref[...] * offsets_ref[...])

    def block(step, _):
        distance = distance_ref[...] + (step * L).astype(jnp.int16)
        inside = (distance >= 0) & (distance < L)
        none = jnp.zeros(base_high.shape, jnp.bfloat16)
        rows = pl.ds(pl.multiple_of(step * L, L), L)
        high_ref[rows, :] = jnp.where(inside, base_high[...], none)
        low_ref[rows, :] = jnp.where(inside, base_low[...], none)
        return 0

    lax.fori_loop(0, high_ref.shape[0] // L, block, 0)


def tables(offsets, frequency, blocks):
    count, groups = offsets.shape[0], frequency.shape[0]
    weights = kept((blocks * L, count), jnp.bfloat16)
    theta = kept((groups, L), jnp.float32)
    phi = kept((groups, count), jnp.float32)
    return pl.pallas_call(
        tables_kernel,
        out_shape=(weights, weights, theta, theta, phi, phi),
        in_specs=[VMEM, VMEM],
        out_specs=(VMEM,) * 6,
        scratch_shapes=[pltpu.VMEM((L, count), kind) for kind in (jnp.int16, jnp.bfloat16, jnp.bfloat16)],
        compiler_params=PARAMS,
        name="tables",
    )(offsets[None, :], frequency[:, None])


def span_kernel(pieces, groups, start, stop, span, *refs):
    refs = list(refs)
    piece_refs, refs = refs[:pieces], refs[pieces:]
    snaps_ref, cos_ref, sin_ref, wh_ref, wl_ref = refs[:5]
    refs = refs[5:]
    before_ref = refs.pop(0) if start else None
    acc_ref = refs.pop(0)
    head_ref = None if start else refs.pop(0)
    modes_ref, high_ref, low_ref = refs

    at = 0
    for ref in piece_refs:
        modes_ref[at : at + ref.shape[0], :] = ref[...]
        at += ref.shape[0]
    if start:
        acc_ref[...] = before_ref[...]
    sign = signs(L)

    def step(index, first):
        here = pl.ds(pl.multiple_of(index * span, span), span)
        projected = dot(modes_ref[...], snaps_ref[here, :], ((1,), (1,)))
        for g in range(acc_ref.shape[0] // ROWS // 2):
            rows = slice(2 * g * ROWS, (2 * g + 2) * ROWS)
            factors = []
            for f in (2 * g, 2 * g + 1):
                at = groups + f
                factors.append((sign * cos_ref[at : at + 1, :], -sin_ref[at : at + 1, :]))
            for b in range(span // L):
                cols = slice(b * L, (b + 1) * L)
                parts = []
                for u, (cosine, sine) in enumerate(factors):
                    f = 2 * g + u
                    x = projected[f * ROWS : (f + 1) * ROWS, cols]
                    parts.append(cosine * x + sine * pltpu.roll(x, M, 0))
                both = jnp.concatenate(parts, 0)
                if first and b == 0:
                    head_ref[rows, :] = both
                high_ref[rows, cols], low_ref[rows, cols] = split(both)
        part = product3(high_ref[...], low_ref[...], wh_ref[here, :], wl_ref[here, :])
        if first:
            acc_ref[...] = part
        else:
            acc_ref[...] += part

    if not start:
        step(0, True)
    if max(start, 1) < stop:
        lax.fori_loop(max(start, 1), stop, lambda index, _: (step(index, False), 0)[1], 0)


def spans(groups, pieces, snapshots, angles, high, low, start, stop, span, before=None):
    depth = snapshots.shape[1]
    rows = sum(piece.shape[0] for piece in pieces)
    count = high.shape[1]
    acc, head = kept((rows, count), jnp.float32), kept((rows, L), jnp.float32)
    inputs = [*pieces, snapshots, *angles[:2], high, low] + ([before] if start else [])
    return pl.pallas_call(
        functools.partial(span_kernel, len(pieces), groups, start, stop, span),
        out_shape=acc if start else (acc, head),
        in_specs=[VMEM] * len(inputs),
        out_specs=VMEM if start else (VMEM, VMEM),
        scratch_shapes=[pltpu.VMEM((rows, depth), jnp.bfloat16)] + [pltpu.VMEM((rows, span), jnp.bfloat16)] * 2,
        compiler_params=PARAMS,
        name="other_spans" if start else "first_spans",
    )(*hold(*inputs))


def code_kernel(per_dest, parts, place_ref, *refs):
    refs = list(refs)
    acc_refs, halo_refs, refs = refs[:parts], refs[parts : 2 * parts], refs[2 * parts :]
    wh_ref, wl_ref, cos_ref, sin_ref, own_ref, *code_refs, full_ref, turned_ref = refs
    tm_pos, row_pos, shift = place_ref[0], place_ref[1], place_ref[2]
    chunk, count = own_ref.shape
    block = chunk // per_dest
    n_tm = turned_ref.shape[0] // block
    order = arrival(n_tm)
    spot = [order.index(d) for d in range(n_tm)]

    def row_of(distance):
        at = jnp.int32(0)
        for d in range(n_tm):
            at = jnp.where(distance == d, spot[d] * block, at)
        return pl.multiple_of(at, ROWS)

    at = 0
    for ref in halo_refs:
        turned_ref[at : at + ref.shape[0], :] = ref[...]
        at += ref.shape[0]
    at = 0
    last = pl.ds(wh_ref.shape[0] - L, L)
    for p, ref in enumerate(acc_refs):
        rows = ref.shape[0]
        pieces = [turned_ref[pl.ds(row_of(order[at // block + i] ^ shift), block), :] for i in range(rows // block)]
        high, low = split(jnp.concatenate(pieces, 0))
        full_ref[at : at + rows, :] = ref[...] + product3(high, low, wh_ref[last, :], wl_ref[last, :])
        at += rows
    sign = signs(count)
    for f in range(cos_ref.shape[0]):
        rows = slice(f * ROWS, (f + 1) * ROWS)
        x = full_ref[rows, :]
        full_ref[rows, :] = cos_ref[f : f + 1, :] * x - (sign * sin_ref[f : f + 1, :]) * pltpu.roll(x, M, 0)
    lane = lax.broadcasted_iota(jnp.int32, (2 * ROWS, LANES), 1)
    for k in range(len(code_refs) + 1):
        for u in range(per_dest):
            at = row_of(((row_pos ^ k) * per_dest + u) ^ tm_pos)
            for r in range(0, block, 2 * ROWS):
                values = full_ref[pl.ds(pl.multiple_of(at + r, ROWS), 2 * ROWS), :]
                rows = slice(u * block + r, u * block + r + 2 * ROWS)
                if k == 0:
                    own_ref[rows, :] = values
                    continue
                peak = jnp.max(jnp.abs(values), axis=1, keepdims=True)
                power = jnp.ceil(jnp.log2(jnp.maximum(peak * (1.0 / TOP), 2.0**-126)))
                power = jnp.maximum(power, -126.0)
                codes = ((values * jnp.exp2(-power) + MAGIC) - MAGIC).astype(jnp.int32)
                bits = lax.shift_right_logical(jnp.broadcast_to(power.astype(jnp.int32) + 127, lane.shape), lane & 7) & 1
                front = codes[:, :LANES]
                front = jnp.where(lane < 8, (front & -2) | bits, front)
                code_refs[k - 1][rows, :LANES] = front.astype(jnp.int16)
                code_refs[k - 1][rows, LANES:] = codes[:, LANES:].astype(jnp.int16)


def rotate_and_code(place, accs, halos, high, low, angles, chunk, sends, per_dest):
    rows, count = sum(acc.shape[0] for acc in accs), accs[0].shape[1]
    code = kept((chunk, count), jnp.int16)
    return pl.pallas_call(
        functools.partial(code_kernel, per_dest, len(accs)),
        out_shape=(kept((chunk, count), jnp.float32),) + (code,) * sends,
        in_specs=[pl.BlockSpec(memory_space=pltpu.SMEM)] + [VMEM] * (2 * len(accs) + 4),
        out_specs=(VMEM,) * (sends + 1),
        scratch_shapes=[pltpu.VMEM((rows, count), jnp.float32), pltpu.VMEM((rows, L), jnp.float32)],
        compiler_params=PARAMS,
        name="rotate_and_code",
    )(place, *hold(*accs, *halos, high, low, *angles[2:]))


def sum_kernel(per_dest, own_ref, *refs):
    *code_refs, out_ref = refs
    chunk, count = own_ref.shape
    step = 2 * ROWS
    lane = lax.broadcasted_iota(jnp.int32, (step, LANES), 1)
    for r in range(0, chunk, step):
        rows = slice(r, r + step)
        total = own_ref[rows, :]
        for ref in code_refs:
            codes = ref[rows, :].astype(jnp.int32)
            bits = jnp.where(lane < 8, (codes[:, :LANES] & 1) << (lane & 7), 0)
            power = jnp.sum(bits.astype(jnp.float32), axis=1, keepdims=True) - 127.0
            total = total + codes.astype(jnp.float32) * jnp.exp2(power)
        for f in range(step // ROWS):
            for p in range(2):
                at = f * ROWS + p * M
                out_ref[r // ROWS + f, p] = total[at : at + M, :]


def add_up(per_dest, own, codes):
    chunk, count = own.shape
    return pl.pallas_call(
        functools.partial(sum_kernel, per_dest),
        out_shape=jax.ShapeDtypeStruct((chunk // ROWS, 2, M, count), jnp.float32),
        in_specs=[VMEM] * (1 + len(codes)),
        out_specs=VMEM,
        compiler_params=PARAMS,
        name="add_up",
    )(*hold(own, *codes))


def arrival(n_tm):
    return sorted(range(n_tm), key=lambda d: (d.bit_count(), d))


def after(values, earlier):
    return list(lax.optimization_barrier((*values, earlier)))[:-1]


def body(snapshots, spod_modes, freq_index, seg_offsets):
    time_len = snapshots.shape[0]
    tm_pos = lax.axis_index("tm")
    row_pos = lax.axis_index("rows")
    n_tm = lax.axis_size("tm")
    n_rows = lax.axis_size("rows")
    per_device = spod_modes.shape[0]
    groups = n_tm * per_device
    per_dest = n_tm // n_rows
    chunk = per_dest * per_device * ROWS
    span = math.gcd(SPAN, time_len)

    blocks = {0: spod_modes.reshape(per_device * ROWS, spod_modes.shape[3])}
    for d in sorted(range(2, n_tm, 2), key=lambda d: d.bit_count()):
        blocks[d] = swap(blocks[0], "tm", d)
    for d in range(0, n_tm, 2):
        blocks[d + 1] = swap(blocks[d], "tm", 1)

    order = arrival(n_tm)
    frequency = freq_index.reshape(n_tm, per_device)[jnp.array(order, jnp.int32) ^ tm_pos].reshape(groups)
    place = jnp.stack([tm_pos, row_pos, (tm_pos ^ (tm_pos + 1)) & (n_tm - 1)]).astype(jnp.int32)
    high, low, *angles = tables(seg_offsets, frequency, time_len // L + 1)
    [snapshots] = after([snapshots], place)

    steps = time_len // span
    route = [(i + 1, i) for i in range(n_tm - 1)]
    half = n_tm // 2
    pieces = [[blocks[d] for d in order[:half]], [blocks[d] for d in order[half:]]]
    first_acc, first_head = spans(0, pieces[0], snapshots, angles, high, low, 0, steps, span)
    pieces[1] = after(pieces[1], first_head)
    first_halo = lax.ppermute(first_head, "tm", route)
    at = half * per_device
    acc, head = spans(at, pieces[1], snapshots, angles, high, low, 0, 1, span)
    halo = lax.ppermute(head, "tm", route)
    acc = spans(at, pieces[1], snapshots, angles, high, low, 1, steps, span, before=acc)
    own, *codes = rotate_and_code(
        place, [first_acc, acc], [first_halo, halo], high, low, angles, chunk, n_rows - 1, per_dest
    )
    return add_up(per_dest, own, [swap(code, "rows", k + 1) for k, code in enumerate(codes)])


def solution(mesh):
    placed = (P("tm", "rows"), P("tm", None, None, "rows"), P(), P("tm"))
    return jax.shard_map(
        body, mesh=mesh, in_specs=placed, out_specs=P("rows", None, None, "tm"), check_vma=False
    )
```

```python
import functools
import math

import jax
import jax.numpy as jnp
from jax import lax
from jax.experimental import pallas as pl
from jax.experimental.pallas import tpu as pltpu
from jax.sharding import PartitionSpec as P


M = 4
L = 256
ROWS = 2 * M
TOP = 32000.0
SPAN = 512
LANES = 128
MAGIC = 12582912.0


def swap(block, axis, distance):
    return lax.ppermute(block, axis, [(i, i ^ distance) for i in range(lax.axis_size(axis))])


def split(value):
    high = value.astype(jnp.bfloat16)
    return high, (value - high.astype(jnp.float32)).astype(jnp.bfloat16)


def dot(a, b, contract=((1,), (0,))):
    return lax.dot_general(a, b, (contract, ((), ())), preferred_element_type=jnp.float32)


def product3(data_high, data_low, weights_high, weights_low):
    return dot(data_high, weights_high) + dot(data_low, weights_high) + dot(data_high, weights_low)


def signs(width):
    real = lax.broadcasted_iota(jnp.int32, (ROWS, width), 0) < M
    return jnp.where(real, 1.0, -1.0).astype(jnp.float32)


VMEM = pl.BlockSpec(memory_space=pltpu.VMEM)
PARAMS = pltpu.CompilerParams(vmem_limit_bytes=20 * 2**20)


def kept(shape, kind):
    return pltpu.VMEM(shape, kind)


def hold(*values):
    return [pltpu.with_memory_space_constraint(value, pltpu.VMEM) for value in values]


def half_sine(phase_bin):
    centred = ((phase_bin + L // 2) & (L - 1)) - L // 2
    u = centred.astype(jnp.float32) * (math.pi / L)
    square = u * u
    sine = jnp.full_like(u, -1.0 / math.factorial(11))
    for k in (9, 7, 5, 3, 1):
        sine = sine * square + (-1.0) ** (k // 2) / math.factorial(k)
    return u, square, u * sine


def cos_sin(phase_bin):
    u, square, sine = half_sine(phase_bin)
    cosine = jnp.full_like(u, 1.0 / math.factorial(12))
    for k in (10, 8, 6, 4, 2, 0):
        cosine = cosine * square + (-1.0) ** (k // 2) / math.factorial(k)
    return 1.0 - 2.0 * sine * sine, 2.0 * sine * cosine


def prep_kernel(frequency_ref, snaps_ref, offsets_ref, *refs):
    out_ref, high_ref, low_ref, cos_ref, sin_ref, seg_cos_ref, seg_sin_ref = refs[:7]
    distance_ref, base_high, base_low, arrived = refs[7:]
    load = pltpu.make_async_copy(snaps_ref, out_ref, arrived)
    load.start()
    shape = base_high.shape
    distance = lax.broadcasted_iota(jnp.int32, shape, 0) - offsets_ref[...]
    _, _, sine = half_sine(distance)
    base_high[...], base_low[...] = split(math.sqrt(8.0 / (3.0 * L)) * (sine * sine))
    distance_ref[...] = distance.astype(jnp.int16)

    tm_pos = lax.axis_index("tm")
    groups, count = seg_cos_ref.shape
    n_tm = lax.axis_size("tm")
    each = groups // n_tm
    row = lax.broadcasted_iota(jnp.int32, (groups, LANES), 0)
    frequency = jnp.zeros((groups, LANES), jnp.int32)
    for i, d in enumerate(arrival(n_tm)):
        for f in range(each):
            frequency = jnp.where(row == i * each + f, frequency_ref[(d ^ tm_pos) * each + f], frequency)
    for at in range(0, L, LANES):
        cols = slice(at, at + LANES)
        moment = lax.broadcasted_iota(jnp.int32, (groups, LANES), 1) + at
        cos_ref[:, cols], sin_ref[:, cols] = cos_sin(frequency * moment)
    for at in range(0, count, LANES):
        cols = slice(at, at + LANES)
        seg_cos_ref[:, cols], seg_sin_ref[:, cols] = cos_sin(frequency * offsets_ref[:, cols])

    def block(step, _):
        distance = distance_ref[...] + (step * L).astype(jnp.int16)
        inside = (distance >= 0) & (distance < L)
        none = jnp.zeros(base_high.shape, jnp.bfloat16)
        rows = pl.ds(pl.multiple_of(step * L, L), L)
        high_ref[rows, :] = jnp.where(inside, base_high[...], none)
        low_ref[rows, :] = jnp.where(inside, base_low[...], none)
        return 0

    lax.fori_loop(0, high_ref.shape[0] // L, block, 0)
    load.wait()


def prep(snapshots, offsets, frequency, blocks):
    count, groups = offsets.shape[0], frequency.shape[0]
    weights = kept((blocks * L, count), jnp.bfloat16)
    theta = kept((groups, L), jnp.float32)
    phi = kept((groups, count), jnp.float32)
    return pl.pallas_call(
        prep_kernel,
        out_shape=(kept(snapshots.shape, snapshots.dtype), weights, weights, theta, theta, phi, phi),
        in_specs=[pl.BlockSpec(memory_space=pltpu.SMEM), pl.BlockSpec(memory_space=pltpu.HBM), VMEM],
        out_specs=(VMEM,) * 7,
        scratch_shapes=[pltpu.VMEM((L, count), kind) for kind in (jnp.int16, jnp.bfloat16, jnp.bfloat16)]
        + [pltpu.SemaphoreType.DMA],
        compiler_params=PARAMS,
        name="prep",
    )(frequency, pltpu.with_memory_space_constraint(snapshots, pltpu.HBM), offsets[None, :])


def span_kernel(pieces, groups, start, stop, span, *refs):
    refs = list(refs)
    piece_refs, refs = refs[:pieces], refs[pieces:]
    snaps_ref, cos_ref, sin_ref, wh_ref, wl_ref = refs[:5]
    refs = refs[5:]
    before_ref = refs.pop(0) if start else None
    acc_ref = refs.pop(0)
    head_ref = None if start else refs.pop(0)
    modes_ref, high_ref, low_ref = refs

    at = 0
    for ref in piece_refs:
        modes_ref[at : at + ref.shape[0], :] = ref[...]
        at += ref.shape[0]
    if start:
        acc_ref[...] = before_ref[...]
    sign = signs(L)

    def step(index, first):
        here = pl.ds(pl.multiple_of(index * span, span), span)
        projected = dot(modes_ref[...], snaps_ref[here, :], ((1,), (1,)))
        for g in range(acc_ref.shape[0] // ROWS // 2):
            rows = slice(2 * g * ROWS, (2 * g + 2) * ROWS)
            factors = []
            for f in (2 * g, 2 * g + 1):
                at = groups + f
                factors.append((sign * cos_ref[at : at + 1, :], -sin_ref[at : at + 1, :]))
            for b in range(span // L):
                cols = slice(b * L, (b + 1) * L)
                parts = []
                for u, (cosine, sine) in enumerate(factors):
                    f = 2 * g + u
                    x = projected[f * ROWS : (f + 1) * ROWS, cols]
                    parts.append(cosine * x + sine * pltpu.roll(x, M, 0))
                both = jnp.concatenate(parts, 0)
                if first and b == 0:
                    head_ref[rows, :] = both
                high_ref[rows, cols], low_ref[rows, cols] = split(both)
        part = product3(high_ref[...], low_ref[...], wh_ref[here, :], wl_ref[here, :])
        if first:
            acc_ref[...] = part
        else:
            acc_ref[...] += part

    if not start:
        step(0, True)
    if max(start, 1) < stop:
        lax.fori_loop(max(start, 1), stop, lambda index, _: (step(index, False), 0)[1], 0)


def spans(groups, pieces, snapshots, angles, high, low, start, stop, span, before=None):
    depth = snapshots.shape[1]
    rows = sum(piece.shape[0] for piece in pieces)
    count = high.shape[1]
    acc, head = kept((rows, count), jnp.float32), kept((rows, L), jnp.float32)
    inputs = [*pieces, snapshots, *angles[:2], high, low] + ([before] if start else [])
    return pl.pallas_call(
        functools.partial(span_kernel, len(pieces), groups, start, stop, span),
        out_shape=acc if start else (acc, head),
        in_specs=[VMEM] * len(inputs),
        out_specs=VMEM if start else (VMEM, VMEM),
        scratch_shapes=[pltpu.VMEM((rows, depth), jnp.bfloat16)] + [pltpu.VMEM((rows, span), jnp.bfloat16)] * 2,
        compiler_params=PARAMS,
        name="other_spans" if start else "first_spans",
    )(*hold(*inputs))


def code_kernel(per_dest, parts, *refs):
    refs = list(refs)
    acc_refs, halo_refs, refs = refs[:parts], refs[parts : 2 * parts], refs[2 * parts :]
    wh_ref, wl_ref, cos_ref, sin_ref, own_ref, *code_refs, full_ref, turned_ref = refs
    tm_pos, row_pos = lax.axis_index("tm"), lax.axis_index("rows")
    chunk, count = own_ref.shape
    block = chunk // per_dest
    n_tm = lax.axis_size("tm")
    shift = (tm_pos ^ (tm_pos + 1)) & (n_tm - 1)
    order = arrival(n_tm)
    spot = [order.index(d) for d in range(n_tm)]

    def row_of(distance):
        at = jnp.int32(0)
        for d in range(n_tm):
            at = jnp.where(distance == d, spot[d] * block, at)
        return pl.multiple_of(at, ROWS)

    at = 0
    for ref in halo_refs:
        turned_ref[at : at + ref.shape[0], :] = ref[...]
        at += ref.shape[0]
    at = 0
    last = pl.ds(wh_ref.shape[0] - L, L)
    for ref in acc_refs:
        rows = ref.shape[0]
        pieces = [turned_ref[pl.ds(row_of(order[at // block + i] ^ shift), block), :] for i in range(rows // block)]
        high, low = split(jnp.concatenate(pieces, 0))
        full_ref[at : at + rows, :] = ref[...] + product3(high, low, wh_ref[last, :], wl_ref[last, :])
        at += rows
    sign = signs(count)
    for f in range(cos_ref.shape[0]):
        rows = slice(f * ROWS, (f + 1) * ROWS)
        x = full_ref[rows, :]
        full_ref[rows, :] = cos_ref[f : f + 1, :] * x - (sign * sin_ref[f : f + 1, :]) * pltpu.roll(x, M, 0)
    lane = lax.broadcasted_iota(jnp.int32, (2 * ROWS, LANES), 1)
    for k in range(len(code_refs) + 1):
        for u in range(per_dest):
            at = row_of(((row_pos ^ k) * per_dest + u) ^ tm_pos)
            for r in range(0, block, 2 * ROWS):
                values = full_ref[pl.ds(pl.multiple_of(at + r, ROWS), 2 * ROWS), :]
                rows = slice(u * block + r, u * block + r + 2 * ROWS)
                if k == 0:
                    own_ref[rows, :] = values
                    continue
                peak = jnp.max(jnp.abs(values), axis=1, keepdims=True)
                power = jnp.ceil(jnp.log2(jnp.maximum(peak * (1.0 / TOP), 2.0**-126)))
                power = jnp.maximum(power, -126.0)
                codes = ((values * jnp.exp2(-power) + MAGIC) - MAGIC).astype(jnp.int32)
                bits = lax.shift_right_logical(jnp.broadcast_to(power.astype(jnp.int32) + 127, lane.shape), lane & 7) & 1
                front = codes[:, :LANES]
                front = jnp.where(lane < 8, (front & -2) | bits, front)
                code_refs[k - 1][rows, :LANES] = front.astype(jnp.int16)
                code_refs[k - 1][rows, LANES:] = codes[:, LANES:].astype(jnp.int16)


def rotate_and_code(accs, halos, high, low, angles, chunk, sends, per_dest):
    rows, count = sum(acc.shape[0] for acc in accs), accs[0].shape[1]
    code = kept((chunk, count), jnp.int16)
    return pl.pallas_call(
        functools.partial(code_kernel, per_dest, len(accs)),
        out_shape=(kept((chunk, count), jnp.float32),) + (code,) * sends,
        in_specs=[VMEM] * (2 * len(accs) + 4),
        out_specs=(VMEM,) * (sends + 1),
        scratch_shapes=[pltpu.VMEM((rows, count), jnp.float32), pltpu.VMEM((rows, L), jnp.float32)],
        compiler_params=PARAMS,
        name="rotate_and_code",
    )(*hold(*accs, *halos, high, low, *angles[2:]))


def sum_kernel(own_ref, *refs):
    *code_refs, out_ref = refs
    chunk, _ = own_ref.shape
    step = 2 * ROWS
    lane = lax.broadcasted_iota(jnp.int32, (step, LANES), 1)
    for r in range(0, chunk, step):
        rows = slice(r, r + step)
        total = own_ref[rows, :]
        for ref in code_refs:
            codes = ref[rows, :].astype(jnp.int32)
            bits = jnp.where(lane < 8, (codes[:, :LANES] & 1) << (lane & 7), 0)
            power = jnp.sum(bits.astype(jnp.float32), axis=1, keepdims=True) - 127.0
            total = total + codes.astype(jnp.float32) * jnp.exp2(power)
        for f in range(step // ROWS):
            for p in range(2):
                at = f * ROWS + p * M
                out_ref[r // ROWS + f, p] = total[at : at + M, :]


def add_up(own, codes):
    chunk, count = own.shape
    return pl.pallas_call(
        sum_kernel,
        out_shape=jax.ShapeDtypeStruct((chunk // ROWS, 2, M, count), jnp.float32),
        in_specs=[VMEM] * (1 + len(codes)),
        out_specs=VMEM,
        compiler_params=PARAMS,
        name="add_up",
    )(*hold(own, *codes))


def arrival(n_tm):
    return sorted(range(n_tm), key=lambda d: (d.bit_count(), d))


def after(values, earlier):
    return list(lax.optimization_barrier((*values, earlier)))[:-1]


def body(snapshots, spod_modes, freq_index, seg_offsets):
    time_len = snapshots.shape[0]
    n_tm = lax.axis_size("tm")
    n_rows = lax.axis_size("rows")
    per_device = spod_modes.shape[0]
    per_dest = n_tm // n_rows
    chunk = per_dest * per_device * ROWS
    span = math.gcd(SPAN, time_len)
    steps = time_len // span

    mine = spod_modes.reshape(per_device * ROWS, spod_modes.shape[3])
    blocks = {0: mine}
    chips = sorted(range(2, n_tm, 2), key=lambda d: d.bit_count())
    for d in chips:
        if d.bit_count() > 1:
            mine, *near = lax.optimization_barrier((mine, *(blocks[e] for e in chips if e.bit_count() < d.bit_count())))
            blocks.update(zip([e for e in chips if e.bit_count() < d.bit_count()], near))
        blocks[d] = swap(mine, "tm", d)
    for d in range(0, n_tm, 2):
        blocks[d + 1] = swap(blocks[d], "tm", 1)

    snapshots, high, low, *angles = prep(snapshots, seg_offsets, freq_index, time_len // L + 1)

    order = arrival(n_tm)
    route = [(i + 1, i) for i in range(n_tm - 1)]
    half = n_tm // 2
    pieces = [[blocks[d] for d in order[:half]], [blocks[d] for d in order[half:]]]
    first_acc, first_head = spans(0, pieces[0], snapshots, angles, high, low, 0, steps, span)
    pieces[1] = after(pieces[1], first_head)
    first_halo = lax.ppermute(first_head, "tm", route)
    at = half * per_device
    acc, head = spans(at, pieces[1], snapshots, angles, high, low, 0, 1, span)
    halo = lax.ppermute(head, "tm", route)
    acc = spans(at, pieces[1], snapshots, angles, high, low, 1, steps, span, before=acc)
    own, *codes = rotate_and_code([first_acc, acc], [first_halo, halo], high, low, angles, chunk, n_rows - 1, per_dest)
    return add_up(own, [swap(code, "rows", k + 1) for k, code in enumerate(codes)])


def solution(mesh):
    placed = (P("tm", "rows"), P("tm", None, None, "rows"), P(), P("tm"))
    return jax.shard_map(body, mesh=mesh, in_specs=placed, out_specs=P("rows", None, None, "tm"), check_vma=False)
```

```python
import functools
import math

import jax
import jax.numpy as jnp
from jax import lax
from jax.experimental import pallas as pl
from jax.experimental.pallas import tpu as pltpu
from jax.sharding import PartitionSpec as P


M = 4
L = 256
ROWS = 2 * M
TOP = 32000.0
SPAN = 1024
LANES = 128
MAGIC = 12582912.0


def swap(block, axis, distance):
    return lax.ppermute(block, axis, [(i, i ^ distance) for i in range(lax.axis_size(axis))])


def split(value):
    high = value.astype(jnp.bfloat16)
    return high, (value - high.astype(jnp.float32)).astype(jnp.bfloat16)


def dot(a, b, contract=((1,), (0,))):
    return lax.dot_general(a, b, (contract, ((), ())), preferred_element_type=jnp.float32)


def product3(data_high, data_low, weights_high, weights_low):
    return dot(data_high, weights_high) + dot(data_low, weights_high) + dot(data_high, weights_low)


def signs(width):
    real = lax.broadcasted_iota(jnp.int32, (ROWS, width), 0) < M
    return jnp.where(real, 1.0, -1.0).astype(jnp.float32)


VMEM = pl.BlockSpec(memory_space=pltpu.VMEM)
PARAMS = pltpu.CompilerParams(vmem_limit_bytes=20 * 2**20)


def kept(shape, kind):
    return pltpu.VMEM(shape, kind)


def hold(*values):
    return [pltpu.with_memory_space_constraint(value, pltpu.VMEM) for value in values]


def half_sine(phase_bin):
    centred = ((phase_bin + L // 2) & (L - 1)) - L // 2
    u = centred.astype(jnp.float32) * (math.pi / L)
    square = u * u
    sine = jnp.full_like(u, -1.0 / math.factorial(11))
    for k in (9, 7, 5, 3, 1):
        sine = sine * square + (-1.0) ** (k // 2) / math.factorial(k)
    return u, square, u * sine


def cos_sin(phase_bin):
    u, square, sine = half_sine(phase_bin)
    cosine = jnp.full_like(u, 1.0 / math.factorial(12))
    for k in (10, 8, 6, 4, 2, 0):
        cosine = cosine * square + (-1.0) ** (k // 2) / math.factorial(k)
    return 1.0 - 2.0 * sine * sine, 2.0 * sine * cosine


def prep_kernel(frequency_ref, snaps_ref, offsets_ref, *refs):
    out_ref, high_ref, low_ref, cos_ref, sin_ref, seg_cos_ref, seg_sin_ref = refs[:7]
    distance_ref, base_high, base_low, arrived = refs[7:]
    load = pltpu.make_async_copy(snaps_ref, out_ref, arrived)
    load.start()
    shape = base_high.shape
    distance = lax.broadcasted_iota(jnp.int32, shape, 0) - offsets_ref[...]
    _, _, sine = half_sine(distance)
    base_high[...], base_low[...] = split(math.sqrt(8.0 / (3.0 * L)) * (sine * sine))
    distance_ref[...] = distance.astype(jnp.int16)

    tm_pos = lax.axis_index("tm")
    groups, count = seg_cos_ref.shape
    n_tm = lax.axis_size("tm")
    each = groups // n_tm
    row = lax.broadcasted_iota(jnp.int32, (groups, LANES), 0)
    frequency = jnp.zeros((groups, LANES), jnp.int32)
    for i, d in enumerate(arrival(n_tm)):
        for f in range(each):
            frequency = jnp.where(row == i * each + f, frequency_ref[(d ^ tm_pos) * each + f], frequency)
    for at in range(0, L, LANES):
        cols = slice(at, at + LANES)
        moment = lax.broadcasted_iota(jnp.int32, (groups, LANES), 1) + at
        cos_ref[:, cols], sin_ref[:, cols] = cos_sin(frequency * moment)
    for at in range(0, count, LANES):
        cols = slice(at, at + LANES)
        seg_cos_ref[:, cols], seg_sin_ref[:, cols] = cos_sin(frequency * offsets_ref[:, cols])

    def block(step, _):
        distance = distance_ref[...] + (step * L).astype(jnp.int16)
        inside = (distance >= 0) & (distance < L)
        none = jnp.zeros(base_high.shape, jnp.bfloat16)
        rows = pl.ds(pl.multiple_of(step * L, L), L)
        high_ref[rows, :] = jnp.where(inside, base_high[...], none)
        low_ref[rows, :] = jnp.where(inside, base_low[...], none)
        return 0

    lax.fori_loop(0, high_ref.shape[0] // L, block, 0)
    load.wait()


def prep(snapshots, offsets, frequency, blocks):
    count, groups = offsets.shape[0], frequency.shape[0]
    weights = kept((blocks * L, count), jnp.bfloat16)
    theta = kept((groups, L), jnp.float32)
    phi = kept((groups, count), jnp.float32)
    return pl.pallas_call(
        prep_kernel,
        out_shape=(kept(snapshots.shape, snapshots.dtype), weights, weights, theta, theta, phi, phi),
        in_specs=[pl.BlockSpec(memory_space=pltpu.SMEM), pl.BlockSpec(memory_space=pltpu.HBM), VMEM],
        out_specs=(VMEM,) * 7,
        scratch_shapes=[pltpu.VMEM((L, count), kind) for kind in (jnp.int16, jnp.bfloat16, jnp.bfloat16)]
        + [pltpu.SemaphoreType.DMA],
        compiler_params=PARAMS,
        name="prep",
    )(frequency, pltpu.with_memory_space_constraint(snapshots, pltpu.HBM), offsets[None, :])


def gathered(piece_refs, modes_ref):
    at = 0
    for ref in piece_refs:
        modes_ref[at : at + ref.shape[0], :] = ref[...]
        at += ref.shape[0]
    return modes_ref[...]


def demodulated(projected, cos_ref, sin_ref, groups, put):
    sign = signs(L)
    for g in range(projected.shape[0] // ROWS // 2):
        rows = slice(2 * g * ROWS, (2 * g + 2) * ROWS)
        factors = []
        for f in (2 * g, 2 * g + 1):
            at = groups + f
            factors.append((sign * cos_ref[at : at + 1, :], -sin_ref[at : at + 1, :]))
        for b in range(projected.shape[1] // L):
            cols = slice(b * L, (b + 1) * L)
            parts = []
            for u, (cosine, sine) in enumerate(factors):
                f = 2 * g + u
                x = projected[f * ROWS : (f + 1) * ROWS, cols]
                parts.append(cosine * x + sine * pltpu.roll(x, M, 0))
            put(rows, cols, jnp.concatenate(parts, 0))


def span_kernel(pieces, groups, span, with_head, *refs):
    piece_refs, refs = refs[:pieces], refs[pieces:]
    snaps_ref, cos_ref, sin_ref, wh_ref, wl_ref, acc_ref = refs[:6]
    head_ref = refs[6] if with_head else None
    modes_ref, high_ref, low_ref = refs[-3:]
    modes = gathered(piece_refs, modes_ref)

    for index in range(snaps_ref.shape[0] // span):
        here = slice(index * span, (index + 1) * span)

        def put(rows, cols, both):
            if with_head and index == 0 and cols.start == 0:
                head_ref[rows, :] = both
            high_ref[rows, cols], low_ref[rows, cols] = split(both)

        demodulated(dot(modes, snaps_ref[here, :], ((1,), (1,))), cos_ref, sin_ref, groups, put)
        part = product3(high_ref[...], low_ref[...], wh_ref[here, :], wl_ref[here, :])
        if index == 0:
            acc_ref[...] = part
        else:
            acc_ref[...] += part


def spans(groups, pieces, snapshots, angles, high, low, span, with_head):
    depth = snapshots.shape[1]
    rows = sum(piece.shape[0] for piece in pieces)
    acc, head = kept((rows, high.shape[1]), jnp.float32), kept((rows, L), jnp.float32)
    inputs = [*pieces, snapshots, *angles[:2], high, low]
    return pl.pallas_call(
        functools.partial(span_kernel, len(pieces), groups, span, with_head),
        out_shape=(acc, head) if with_head else acc,
        in_specs=[VMEM] * len(inputs),
        out_specs=(VMEM, VMEM) if with_head else VMEM,
        scratch_shapes=[pltpu.VMEM((rows, depth), jnp.bfloat16)] + [pltpu.VMEM((rows, span), jnp.bfloat16)] * 2,
        compiler_params=PARAMS,
        name="spans",
    )(*hold(*inputs))


def encode(values):
    peak = jnp.max(jnp.abs(values), axis=1, keepdims=True)
    power = jnp.ceil(jnp.log2(jnp.maximum(peak * (1.0 / TOP), 2.0**-126)))
    power = jnp.maximum(power, -126.0)
    codes = ((values * jnp.exp2(-power) + MAGIC) - MAGIC).astype(jnp.int32)
    lane = lax.broadcasted_iota(jnp.int32, (values.shape[0], LANES), 1)
    bits = lax.shift_right_logical(jnp.broadcast_to(power.astype(jnp.int32) + 127, lane.shape), lane & 7) & 1
    front = codes[:, :LANES]
    front = jnp.where(lane < 8, (front & -2) | bits, front)
    return front.astype(jnp.int16), codes[:, LANES:].astype(jnp.int16)


def decode(codes):
    codes = codes.astype(jnp.int32)
    lane = lax.broadcasted_iota(jnp.int32, (codes.shape[0], LANES), 1)
    bits = jnp.where(lane < 8, (codes[:, :LANES] & 1) << (lane & 7), 0)
    power = jnp.sum(bits.astype(jnp.float32), axis=1, keepdims=True) - 127.0
    return codes.astype(jnp.float32) * jnp.exp2(power)


def head_kernel(pieces, groups, *refs):
    piece_refs, (snaps_ref, cos_ref, sin_ref, before_ref, code_ref, modes_ref) = refs[:pieces], refs[pieces:]
    start = before_ref.shape[0]
    for r in range(0, start, 2 * ROWS):
        rows = slice(r, r + 2 * ROWS)
        code_ref[rows, :LANES], code_ref[rows, LANES:] = encode(before_ref[rows, :])

    def put(rows, cols, both):
        rows = slice(start + rows.start, start + rows.stop)
        code_ref[rows, :LANES], code_ref[rows, LANES:] = encode(both)

    demodulated(dot(gathered(piece_refs, modes_ref), snaps_ref[:L, :], ((1,), (1,))), cos_ref, sin_ref, groups, put)


def heads(groups, pieces, snapshots, angles, before):
    rows = sum(piece.shape[0] for piece in pieces)
    inputs = [*pieces, snapshots, *angles[:2], before]
    return pl.pallas_call(
        functools.partial(head_kernel, len(pieces), groups),
        out_shape=kept((before.shape[0] + rows, L), jnp.int16),
        in_specs=[VMEM] * len(inputs),
        out_specs=VMEM,
        scratch_shapes=[pltpu.VMEM((rows, snapshots.shape[1]), jnp.bfloat16)],
        compiler_params=PARAMS,
        name="heads",
    )(*hold(*inputs))


def code_kernel(per_dest, parts, *refs):
    refs = list(refs)
    acc_refs, refs = refs[:parts], refs[parts:]
    halo_ref, wh_ref, wl_ref, cos_ref, sin_ref, own_ref, *code_refs, full_ref, turned_ref = refs
    tm_pos, row_pos = lax.axis_index("tm"), lax.axis_index("rows")
    chunk, count = own_ref.shape
    block = chunk // per_dest
    n_tm = lax.axis_size("tm")
    shift = (tm_pos ^ (tm_pos + 1)) & (n_tm - 1)
    order = arrival(n_tm)
    spot = [order.index(d) for d in range(n_tm)]

    def row_of(distance):
        at = jnp.int32(0)
        for d in range(n_tm):
            at = jnp.where(distance == d, spot[d] * block, at)
        return pl.multiple_of(at, 2 * ROWS)

    for i, d in enumerate(order):
        turned_ref[i * block : (i + 1) * block, :] = decode(halo_ref[pl.ds(row_of(d ^ shift), block), :])
    last = slice(wh_ref.shape[0] - L, wh_ref.shape[0])
    at = 0
    for ref in acc_refs:
        rows = slice(at, at + ref.shape[0])
        high, low = split(turned_ref[rows, :])
        full_ref[rows, :] = ref[...] + product3(high, low, wh_ref[last, :], wl_ref[last, :])
        at = rows.stop
    sign = signs(count)
    for f in range(cos_ref.shape[0]):
        rows = slice(f * ROWS, (f + 1) * ROWS)
        x = full_ref[rows, :]
        full_ref[rows, :] = cos_ref[f : f + 1, :] * x - (sign * sin_ref[f : f + 1, :]) * pltpu.roll(x, M, 0)
    for k in range(len(code_refs) + 1):
        for u in range(per_dest):
            at = row_of(((row_pos ^ k) * per_dest + u) ^ tm_pos)
            for r in range(0, block, 2 * ROWS):
                values = full_ref[pl.ds(pl.multiple_of(at + r, ROWS), 2 * ROWS), :]
                rows = slice(u * block + r, u * block + r + 2 * ROWS)
                if k == 0:
                    own_ref[rows, :] = values
                else:
                    code_refs[k - 1][rows, :LANES], code_refs[k - 1][rows, LANES:] = encode(values)


def rotate_and_code(accs, halo, high, low, angles, chunk, sends, per_dest):
    rows, count = sum(acc.shape[0] for acc in accs), accs[0].shape[1]
    code = kept((chunk, count), jnp.int16)
    return pl.pallas_call(
        functools.partial(code_kernel, per_dest, len(accs)),
        out_shape=(kept((chunk, count), jnp.float32),) + (code,) * sends,
        in_specs=[VMEM] * (len(accs) + 5),
        out_specs=(VMEM,) * (sends + 1),
        scratch_shapes=[pltpu.VMEM((rows, count), jnp.float32), pltpu.VMEM((rows, L), jnp.float32)],
        compiler_params=PARAMS,
        name="rotate_and_code",
    )(*hold(*accs, halo, high, low, *angles[2:]))


def sum_kernel(own_ref, *refs):
    *code_refs, out_ref = refs
    chunk, _ = own_ref.shape
    step = 2 * ROWS
    for r in range(0, chunk, step):
        rows = slice(r, r + step)
        total = own_ref[rows, :]
        for ref in code_refs:
            total = total + decode(ref[rows, :])
        for f in range(step // ROWS):
            for p in range(2):
                at = f * ROWS + p * M
                out_ref[r // ROWS + f, p] = total[at : at + M, :]


def add_up(own, codes):
    chunk, count = own.shape
    return pl.pallas_call(
        sum_kernel,
        out_shape=jax.ShapeDtypeStruct((chunk // ROWS, 2, M, count), jnp.float32),
        in_specs=[VMEM] * (1 + len(codes)),
        out_specs=VMEM,
        compiler_params=PARAMS,
        name="add_up",
    )(*hold(own, *codes))


def arrival(n_tm):
    return sorted(range(n_tm), key=lambda d: (d.bit_count(), d))


def after(values, earlier):
    return list(lax.optimization_barrier((*values, earlier)))[:-1]


def body(snapshots, spod_modes, freq_index, seg_offsets):
    time_len = snapshots.shape[0]
    n_tm = lax.axis_size("tm")
    n_rows = lax.axis_size("rows")
    per_device = spod_modes.shape[0]
    per_dest = n_tm // n_rows
    chunk = per_dest * per_device * ROWS
    span = math.gcd(SPAN, time_len)

    mine = spod_modes.reshape(per_device * ROWS, spod_modes.shape[3])
    blocks = {0: mine}
    chips = sorted(range(2, n_tm, 2), key=lambda d: d.bit_count())
    for d in chips:
        if d.bit_count() > 1:
            mine, *near = lax.optimization_barrier((mine, *(blocks[e] for e in chips if e.bit_count() < d.bit_count())))
            blocks.update(zip([e for e in chips if e.bit_count() < d.bit_count()], near))
        blocks[d] = swap(mine, "tm", d)
    for d in range(0, n_tm, 2):
        blocks[d + 1] = swap(blocks[d], "tm", 1)

    snapshots, high, low, *angles = prep(snapshots, seg_offsets, freq_index, time_len // L + 1)

    order = arrival(n_tm)
    route = [(i + 1, i) for i in range(n_tm - 1)]
    half = n_tm // 2
    pieces = [[blocks[d] for d in order[:half]], [blocks[d] for d in order[half:]]]
    first_acc, first_head = spans(0, pieces[0], snapshots, angles, high, low, span, True)
    pieces[1] = after(pieces[1], first_head)
    at = half * per_device
    codes = heads(at, pieces[1], snapshots, angles, first_head)
    halo = lax.ppermute(codes, "tm", route)
    [snapshots] = after([snapshots], codes)
    acc = spans(at, pieces[1], snapshots, angles, high, low, span, False)
    own, *codes = rotate_and_code([first_acc, acc], halo, high, low, angles, chunk, n_rows - 1, per_dest)
    for k, code in enumerate(codes):
        codes[k] = swap(code, "rows", k + 1)
    return add_up(own, codes)


def solution(mesh):
    placed = (P("tm", "rows"), P("tm", None, None, "rows"), P(), P("tm"))
    return jax.shard_map(body, mesh=mesh, in_specs=placed, out_specs=P("rows", None, None, "tm"), check_vma=False)
```
